32 devices in a mesh: level: 8 (over y, x, core), row: 4 (over z).
Axes of the slice: x: 2, y: 2, z: 4, core: 2. Of those that a mesh axis runs over, the one named last changes fastest.
Arguments:
- right_side: float32 [64, 32, 128], P('level'), may hold values from -6 to 6
- inverses: float32 [64, 128, 128], P('level'), as said below
- blocks: float32 [64, 8, 128, 128], P('level', 'row'), may hold values from -0.125 to 0.125
- sources: int32 [64, 8], P('level', 'row'), may hold values from -1 to 55, as said below
Outputs:
- solved: float32 [64, 32, 128], P('level')
The draws below stay inside these ranges and needn't reach their ends.
Inputs may be any that keep to these rules, and one draw needn't show every extreme that they name: `sources`: the supernodes form an elimination tree: every supernode below the top level has one parent on the next level, and every supernode above level 0 has exactly one child. The entries of supernode t are its 8 highest-numbered descendants in that tree, distinct and in falling order, followed by -1 for empty slots; the supernodes of level 0 have only empty slots. `inverses`: lower triangular.
All inputs are finite; a program needn't handle non-finite values.
Results may differ from the reference program's by a relative error of at most 0.0001.
Values sent between devices are 32-bit elements; how exact they have to be, the bound alone decides.
No kernel may reach another device: no remote copies, remote signals or barrier semaphores. Data moves between devices by JAX's collectives and lax.ppermute only.
A program may use at most 64 MiB of HBM per device.

```python
import math
import jax
import jax.numpy as jnp
from jax import lax

W = 128
NRHS = 32
SN_DEV = 8
SUPERNODES = 64
SLOTS = 8
N_LEVEL = 8


def draw_sources(key, part):
    nodes = jnp.arange(SUPERNODES, dtype=jnp.int32)
    level_of = nodes // SN_DEV
    level_keys = jax.random.split(jax.random.fold_in(key, 5), N_LEVEL)
    orders = jax.vmap(lambda k: jax.random.permutation(k, SN_DEV))(level_keys).astype(jnp.int32)
    offset = orders.reshape(SUPERNODES)
    parent = jnp.where(level_of < N_LEVEL - 1, (level_of + 1) * SN_DEV + offset, -1).astype(jnp.int32)
    current = parent
    below = jnp.zeros((SUPERNODES, SUPERNODES), jnp.int32)
    for step in range(N_LEVEL):
        below = jnp.maximum(below, (current[None, :] == nodes[:, None]).astype(jnp.int32))
        stepped = parent[jnp.maximum(current, 0)]
        current = jnp.where(current >= 0, stepped, -1).astype(jnp.int32)
    scores = jnp.where(below > 0, nodes[None, :], -1).astype(jnp.int32)
    values, places = lax_top(scores)
    return values.astype(jnp.int32)


def lax_top(scores):
    return jax.lax.top_k(scores, SLOTS)


def draw_inverses(key, part):
    key_diag = jax.random.fold_in(key, 11)
    key_off = jax.random.fold_in(key, 23)
    index = jnp.arange(W)
    lower = index[:, None] > index[None, :]
    same = index[:, None] == index[None, :]
    diagonal = jax.random.uniform(key_diag, (SUPERNODES, W), jnp.float32, 0.5, 1.5)
    offdiag = jax.random.normal(key_off, (SUPERNODES, W, W), jnp.float32) * (0.6 / math.sqrt(W))
    filled = jnp.where(lower[None, :, :], offdiag, 0.0)
    return jnp.where(same[None, :, :], diagonal[:, :, None], filled).astype(jnp.float32)


def steps_of(rng, dims, cuts, least, top_value):
    level = 1.0
    for axis_at, blocks in cuts:
        draws = jax.random.uniform(jax.random.fold_in(jax.random.fold_in(rng, 6), axis_at), (blocks,), jnp.float32, least / len(cuts), top_value / len(cuts))
        level = level * jnp.repeat(jnp.exp(draws), dims[axis_at] // blocks).reshape((-1,) + (1,) * (len(dims) - 1 - axis_at))
    return level


def bell_draw(own_key, shape, width, most, pieces=(), kind=jnp.bfloat16):
    drawn = jax.random.normal(own_key, shape, jnp.float32) * width
    if len(pieces) > 0:
        drawn = steps_of(own_key, shape, pieces, -0.22, 0.18) * drawn
    return jnp.clip(drawn, min=-most, max=most).astype(kind)


def setup_inputs(seed: int = 0) -> dict:
    keys = jax.random.split(jax.random.key(seed), 5)
    right_side = bell_draw(keys[0], (SUPERNODES, NRHS, W), 1.0, 6.0, ((0, 8),), jnp.float32)
    inverses = draw_inverses(jax.random.fold_in(keys[4], 71), 0)
    blocks = bell_draw(keys[2], (SUPERNODES, SLOTS, W, W), (2 * SLOTS * W) ** -0.5, 0.125, ((0, 8), (1, 4)), jnp.float32)
    sources = draw_sources(jax.random.fold_in(keys[4], 71), 0)
    return dict(right_side=right_side, inverses=inverses, blocks=blocks, sources=sources)


def reference(right_side, inverses, blocks, sources):
    highest = lax.Precision.HIGHEST
    solved = jnp.zeros((SUPERNODES, NRHS, W), jnp.float32)
    for level_now in range(N_LEVEL):
        first = level_now * SN_DEV
        level_sources = sources[first:first + SN_DEV]
        valid = (level_sources >= 0).astype(jnp.float32)
        picked = solved[jnp.maximum(level_sources, 0).astype(jnp.int32)] * valid[:, :, None, None]
        updates = jnp.einsum("srnw,srwv->snv", picked, blocks[first:first + SN_DEV], precision=highest)
        residue = right_side[first:first + SN_DEV] - updates
        result = jnp.einsum("snw,svw->snv", residue, inverses[first:first + SN_DEV], precision=highest)
        solved = solved.at[first:first + SN_DEV].set(result)
    return solved
```

```python
import functools

import jax
import jax.numpy as jnp
from jax import lax
from jax.experimental import pallas as pl
from jax.experimental.pallas import tpu as pltpu
from jax.sharding import PartitionSpec as P


F32 = jnp.float32
I32 = jnp.int32


def dot(x, w, dims=((1,), (0,))):
    return lax.dot_general(x, w, (dims, ((), ())), precision=lax.Precision.HIGHEST, preferred_element_type=F32)


def dot_t(x, w):
    return dot(x, w, ((1,), (1,)))


def emit(i, n, half, rows, msg, nat, ta, tb, xa, xb):
    msg[pl.ds(i * rows, rows), :] = xa
    msg[pl.ds((half + i) * rows, rows), :] = xb
    msg[pl.ds(2 * half * rows + i, 1), :] = jnp.broadcast_to(tb.astype(F32), (1, xa.shape[1]))
    nat[0, ta] = xa
    nat[1, tb] = xb


def first_kernel(n, half, rows, info, down, inv0, inv1, blk0, blk1, rhs0, rhs1, msg, nat):
    member = info[0]
    nat[...] = jnp.zeros_like(nat)
    msg[...] = jnp.zeros_like(msg)

    def run(inv_a, inv_b, blk_b, rhs_a, rhs_b):
        for i in range(half):
            tb = member * half + i
            ta = down[tb]
            xa = dot_t(rhs_a[ta], inv_a[ta])
            xb = dot_t(rhs_b[tb] - dot(xa, blk_b[tb, 0]), inv_b[tb])
            emit(i, n, half, rows, msg, nat, ta, tb, xa, xb)

    @pl.when(jnp.logical_and(info[1] == 1, member == 0))
    def _():
        run(inv0, inv1, blk1, rhs0, rhs1)

    @pl.when(jnp.logical_and(info[1] == 1, member == 1))
    def _():
        run(inv1, inv0, blk0, rhs1, rhs0)


def step_kernel(n, half, rows, count, info, up, *refs):
    member, active, solver = info[0], info[1], info[2]
    xs = refs[:count]
    acc_in, msg_in, nat_in = refs[count:count + 3]
    inv0, inv1, blk0, blk1, pre0, pre1, rhs0, rhs1, msg, nat = refs[count + 3:]

    @pl.when(active == 0)
    def _():
        msg[...] = msg_in[...]
        nat[...] = nat_in[...]

    def arrived(start, size):
        total = xs[0][pl.ds(start, size), :]
        for x in xs[1:]:
            total = total + x[pl.ds(start, size), :]
        return total

    def run(inv_a, inv_b, blk_a, blk_b, pre, rhs_a, rhs_b):
        nat[...] = jnp.zeros_like(nat)
        msg[...] = jnp.zeros_like(msg)
        ids = arrived(2 * half * rows, 8)
        for i in range(half):
            child = jnp.max(ids[i:i + 1]).astype(I32)
            ta, tb = up[0, child], up[1, child]
            sa, sb = arrived(i * rows, rows), arrived((half + i) * rows, rows)
            ua = acc_in[pl.ds(i * rows, rows), :] + dot(sa, blk_a[ta, 1]) + dot(sb, blk_a[ta, 0])
            ub = acc_in[pl.ds((half + i) * rows, rows), :] + dot(sa, pre[tb]) + dot(sb, blk_b[tb, 1])

            @pl.when(solver == 1)
            def _():
                xa = dot_t(rhs_a[ta] - ua, inv_a[ta])
                xb = dot_t(rhs_b[tb] - ub - dot(xa, blk_b[tb, 0]), inv_b[tb])
                emit(i, n, half, rows, msg, nat, ta, tb, xa, xb)

            @pl.when(solver == 0)
            def _():
                msg[pl.ds(i * rows, rows), :] = ua
                msg[pl.ds((half + i) * rows, rows), :] = ub

    @pl.when(jnp.logical_and(active == 1, member == 0))
    def _():
        run(inv0, inv1, blk0, blk1, pre1, rhs0, rhs1)

    @pl.when(jnp.logical_and(active == 1, member == 1))
    def _():
        run(inv1, inv0, blk1, blk0, pre0, rhs1, rhs0)


def call(kernel, n_smem, n_vmem, shapes):
    return pl.pallas_call(
        kernel,
        out_shape=shapes,
        in_specs=[pl.BlockSpec(memory_space=pltpu.SMEM)] * n_smem + [pl.BlockSpec(memory_space=pltpu.VMEM)] * n_vmem,
        out_specs=[pl.BlockSpec(memory_space=pltpu.VMEM)] * len(shapes),
        compiler_params=pltpu.CompilerParams(vmem_limit_bytes=32 * 1024 * 1024),
    )


def per_device(right_side, inverses, blocks, sources):
    n, rows, w = right_side.shape
    half = n // 2
    levels, planes = lax.axis_size("level"), lax.axis_size("row")
    stages = levels // 2
    level, plane = lax.axis_index("level"), lax.axis_index("row")
    member, stage = level % 2, level // 2

    def move(value, pairs):
        return lax.ppermute(value, ("level", "row"), [(a * planes + b, c * planes + d) for (a, b), (c, d) in pairs])

    def other(value):
        return lax.ppermute(value, "level", [(i, i ^ 1) for i in range(levels)])

    lower = [((l, p + 1), (l, p)) for l in range(3, levels, 2) for p in range(min(planes - 1, l // 2))]
    pre = move(blocks[:, 0], lower)

    sources_o = other(sources)
    inv_o, blk_o, rhs_o = other(inverses), other(blocks), other(right_side)

    src_a = jnp.where(member == 0, sources, sources_o)
    src_b = jnp.where(member == 0, sources_o, sources)
    offset = jnp.arange(n, dtype=I32)

    down = src_b[:, 0] % n
    info = jnp.stack([member, jnp.logical_and(stage == 0, plane == 0).astype(I32)]).astype(I32)
    shapes = [jax.ShapeDtypeStruct((2 * half * rows + 8, w), F32), jax.ShapeDtypeStruct((2, n, rows, w), F32)]
    msg, nat = call(functools.partial(first_kernel, n, half, rows), 2, 6, shapes)(
        info, jnp.clip(down, 0, n - 1), inverses, inv_o, blocks, blk_o, right_side, rhs_o)

    def inverse_map(column):
        hit = jnp.logical_and(column[:, None] >= 0, column[:, None] % n == offset[None, :])
        return jnp.sum(jnp.where(hit, offset[:, None], 0), axis=0).astype(I32)

    up = jnp.stack([inverse_map(src_a[:, 0]), inverse_map(src_b[:, 1])])
    pre_o = other(pre)
    acc = jnp.zeros_like(msg)
    for g in range(stages - 1):
        xs = [move(msg, [((2 * g + m, 0), (2 * (g + d) + m, d - 1)) for m in (0, 1)]) for d in range(1, stages - g)]
        back = [((2 * h + m, h - g), (2 * h + m, h - g - 1)) for h in range(g + 1, stages) for m in (0, 1)] if g else []
        if back:
            acc = move(msg, back)
        info = jnp.stack([member, (stage - 1 - plane == g).astype(I32), (plane == 0).astype(I32)]).astype(I32)
        msg, nat = call(functools.partial(step_kernel, n, half, rows, len(xs)), 2, len(xs) + 11, shapes)(
            info, up, *xs, acc, msg, nat, inverses, inv_o, blocks, blk_o, pre, pre_o, right_side, rhs_o)

    mine = lax.dynamic_index_in_dim(nat, member, 0, keepdims=False)
    theirs = lax.dynamic_index_in_dim(nat, 1 - member, 0, keepdims=False)
    solved = mine + other(theirs)
    out = jnp.where(plane == 0, solved, 0)
    for q in range(1, planes):
        out = out + move(solved, [((l, 0), (l, q)) for l in range(levels)])
    return out


def solution(mesh):
    return jax.shard_map(
        per_device,
        mesh=mesh,
        in_specs=(
            P("level", None, None),
            P("level", None, None),
            P("level", "row", None, None),
            P("level", "row"),
        ),
        out_specs=P("level", None, None),
        check_vma=False,
    )
```

```python
import functools

import jax
import jax.numpy as jnp
from jax import lax
from jax.experimental import pallas as pl
from jax.experimental.pallas import tpu as pltpu
from jax.sharding import PartitionSpec as P


F32 = jnp.float32
BF16 = jnp.bfloat16
I32 = jnp.int32


def position():
    level = lax.axis_index("level")
    return lax.rem(level, 2), lax.div(level, 2), lax.axis_index("row")


def split(v):
    high = v.astype(BF16)
    return high, (v - high.astype(F32)).astype(BF16)


def product(xs, ws, transposed=False):
    dims = (((1,), (1 if transposed else 0,)), ((), ()))
    parts = [(split(x), split(w)) for x, w in zip(xs, ws)]
    mul = lambda x, w: lax.dot_general(x, w, dims, preferred_element_type=F32)
    out = []
    for (xh, xl), (wh, wl) in parts:
        both = mul(jnp.concatenate([xh, xl], 0), wh)
        rows = xh.shape[0]
        out.append(both[:rows] + both[rows:] + mul(xh, wl))
    return out


def plus(xs, ys):
    return [x + y for x, y in zip(xs, ys)]


def emit(half, rows, msg, tb, xa, xb):
    for i in range(half):
        msg[pl.ds(i * rows, rows), :] = xa[i]
        msg[pl.ds((half + i) * rows, rows), :] = xb[i]
        msg[pl.ds(2 * half * rows + i, 1), :] = jnp.full((1, xa[i].shape[1]), tb[i], I32).astype(F32)


def load_kernel(n, rows, inv_h, blk_h, rhs_h, inv, blk, rhs, first, x0, sems):
    member, stage, _ = position()
    copies = [
        pltpu.make_async_copy(inv_h, inv, sems.at[0]),
        pltpu.make_async_copy(rhs_h, rhs, sems.at[1]),
        pltpu.make_async_copy(blk_h, blk, sems.at[2]),
    ]
    for copy in copies:
        copy.start()
    copies[0].wait()
    copies[1].wait()

    @pl.when(jnp.logical_and(stage == 0, member == 0))
    def _():
        for i, x in enumerate(product([rhs[t] for t in range(n)], [inv[t] for t in range(n)], True)):
            x0[pl.ds(i * rows, rows), :] = x

    copies[2].wait()
    for t in range(n):
        first[t] = blk[t, 0]


def scatter(n, source, column, maps, row):
    for t in range(n):
        maps[row, t] = 0
    for t in range(n):
        @pl.when(source[column, t] >= 0)
        def _():
            maps[row, lax.rem(source[column, t], n)] = t


def early_kernel(n, half, rows, own, x0, blk, low, high, place):
    member, stage, plane = position()

    @pl.when(jnp.logical_and(member == 1, stage == plane))
    def _():
        scatter(n, own, 0, place, 0)
        us = product([x0[pl.ds(k * rows, rows), :] for k in range(n)], [blk[place[0, k], 0] for k in range(n)])
        for i in range(half):
            low[pl.ds(i * rows, rows), :] = us[i]
            high[pl.ds(i * rows, rows), :] = us[half + i]


def first_kernel(n, half, rows, own, oth, inv0, inv1, blk0, blk1, rhs0, rhs1, msg, maps):
    member, stage, plane = position()
    active = jnp.logical_and(stage == 0, plane == 0)

    def run(src_b, inv_a, inv_b, blk_b, rhs_a, rhs_b):
        scatter(n, src_b, 0, maps, 0)
        ta = [member * half + i for i in range(half)]
        tb = [maps[0, t] for t in ta]
        xa = product([rhs_a[t] for t in ta], [inv_a[t] for t in ta], True)
        ub = product(xa, [blk_b[t, 0] for t in tb])
        xb = product([rhs_b[t] - u for t, u in zip(tb, ub)], [inv_b[t] for t in tb], True)
        msg[pl.ds(2 * half * rows, 8), :] = jnp.zeros((8, msg.shape[1]), F32)
        emit(half, rows, msg, tb, xa, xb)

    @pl.when(jnp.logical_not(active))
    def _():
        msg[...] = jnp.zeros_like(msg)

    @pl.when(jnp.logical_and(active, member == 0))
    def _():
        run(oth, inv0, inv1, blk1, rhs0, rhs1)

    @pl.when(jnp.logical_and(active, member == 1))
    def _():
        run(own, inv1, inv0, blk0, rhs1, rhs0)


def step_kernel(n, half, rows, g, count, last, own, oth, *refs):
    refs, maps = refs[:-1], refs[-1]
    member, stage, plane = position()
    active, solver = stage - 1 - plane == g, plane == 0
    xs = refs[:count]
    more = refs[count:count + 2]
    msg_in, inv0, inv1, blk0, blk1, rhs0, rhs1 = refs[count + 2:count + 9]
    rest = refs[count + 9:]
    if g:
        acc, (pre0, pre1), rest = more[0], (more[1], rest[0]), rest[1:]
    else:
        pre0 = pre1 = None
    msg, outs = (rest[2], rest[:2]) if last else (rest[0], None)

    @pl.when(jnp.logical_not(active))
    def _():
        msg[...] = msg_in[...]

    def arrived(start, size):
        total = xs[0][pl.ds(start, size), :]
        for x in xs[1:]:
            total = total + x[pl.ds(start, size), :]
        return total

    def run(src_a, src_b, inv_a, inv_b, blk_a, blk_b, pre, rhs_a, rhs_b):
        scatter(n, src_a, 0, maps, 0)
        scatter(n, src_b, 1, maps, 1)
        ids = arrived(2 * half * rows, 8)
        child = [jnp.max(ids[i:i + 1]).astype(I32) for i in range(half)]
        ta, tb = [maps[0, c] for c in child], [maps[1, c] for c in child]
        sa = [arrived(i * rows, rows) for i in range(half)]
        sb = [arrived((half + i) * rows, rows) for i in range(half)]
        ua = plus(product(sa, [blk_a[t, 1] for t in ta]), product(sb, [blk_a[t, 0] for t in ta]))
        ub = product(sb, [blk_b[t, 1] for t in tb])
        if g:
            ua = plus(ua, [acc[pl.ds(i * rows, rows), :] for i in range(half)])
            ub = plus(ub, [acc[pl.ds((half + i) * rows, rows), :] for i in range(half)])
            ub = plus(ub, product(sa, [pre[t] for t in tb]))
        else:
            ub = plus(ub, [more[0][pl.ds(i * rows, rows), :] + more[1][pl.ds(i * rows, rows), :] for i in range(half)])
        msg[pl.ds(2 * half * rows, 8), :] = jnp.zeros((8, msg.shape[1]), F32)

        @pl.when(solver)
        def _():
            xa = product([rhs_a[t] - u for t, u in zip(ta, ua)], [inv_a[t] for t in ta], True)
            vb = plus(ub, product(xa, [blk_b[t, 0] for t in tb]))
            xb = product([rhs_b[t] - v for t, v in zip(tb, vb)], [inv_b[t] for t in tb], True)
            emit(half, rows, msg, tb, xa, xb)

        @pl.when(jnp.logical_not(solver))
        def _():
            emit(half, rows, msg, [0] * half, ua, ub)

    @pl.when(jnp.logical_and(active, member == 0))
    def _():
        run(own, oth, inv0, inv1, blk0, blk1, pre1, rhs0, rhs1)

    @pl.when(jnp.logical_and(active, member == 1))
    def _():
        run(oth, own, inv1, inv0, blk1, blk0, pre0, rhs1, rhs0)

    if last:
        mine, theirs = outs
        mine[...] = jnp.zeros_like(mine)
        theirs[...] = jnp.zeros_like(theirs)

        def place(src_b, out_a, out_b):
            ids = msg[pl.ds(2 * half * rows, 8), :]
            for i in range(half):
                tb = jnp.max(ids[i:i + 1]).astype(I32)
                out_a[lax.rem(jnp.maximum(src_b[0, tb], 0), n)] = msg[pl.ds(i * rows, rows), :]
                out_b[tb] = msg[pl.ds((half + i) * rows, rows), :]

        @pl.when(jnp.logical_and(solver, member == 0))
        def _():
            place(oth, mine, theirs)

        @pl.when(jnp.logical_and(solver, member == 1))
        def _():
            place(own, theirs, mine)


def pick_kernel(*refs):
    _, _, plane = position()
    zs, out, sem = refs[:-2], refs[-2], refs[-1]
    for q, z in enumerate(zs):
        @pl.when(plane == q)
        def _():
            copy = pltpu.make_async_copy(z, out, sem)
            copy.start()
            copy.wait()


SMEM, VMEM, HBM = pltpu.SMEM, pltpu.VMEM, pltpu.HBM


def call(kernel, ins, outs, shapes, scratch=()):
    def run(*args):
        args = [pltpu.with_memory_space_constraint(a, m) if m in (VMEM, HBM) else a for a, m in zip(args, ins)]
        return run_raw(*args)

    run_raw = pl.pallas_call(
        kernel,
        out_shape=shapes,
        in_specs=[pl.BlockSpec(memory_space=s) for s in ins],
        out_specs=[pl.BlockSpec(memory_space=s) for s in outs],
        scratch_shapes=scratch,
        compiler_params=pltpu.CompilerParams(vmem_limit_bytes=4 * 1024 * 1024),
    )
    return run


def solve(right_side, inverses, blocks, sources):
    n, rows, w = right_side.shape
    half = n // 2
    levels, planes = lax.axis_size("level"), lax.axis_size("row")
    stages = levels // 2
    shape = lambda *s: jax.ShapeDtypeStruct(s, F32)

    def move(value, pairs):
        return lax.ppermute(value, ("level", "row"), [(a * planes + b, c * planes + d) for (a, b), (c, d) in pairs])

    def other(value):
        return lax.ppermute(value, "level", [(i, i ^ 1) for i in range(levels)])

    own = sources.T
    oth = other(own)
    inv_o, rhs_o, blk_o = other(inverses), other(right_side), other(blocks)

    inv, blk, rhs, first, x0 = call(
        functools.partial(load_kernel, n, rows), [HBM] * 3, [VMEM] * 5,
        [shape(n, w, w), shape(n, 2, w, w), shape(n, rows, w), shape(n, w, w), shape(n * rows, w)], [pltpu.SemaphoreType.DMA((3,))],
    )(inverses, blocks, right_side)
    x0 = move(x0, [((0, h), (2 * h + 1, h)) for h in range(1, stages)])
    pre = move(first, [((2 * h + 1, p + 1), (2 * h + 1, p)) for h in range(2, stages) for p in range(h - 1)])

    msg_shape = shape(2 * half * rows + 8, w)
    msg, = call(functools.partial(first_kernel, n, half, rows), [SMEM] * 2 + [VMEM] * 6, [VMEM], [msg_shape], [pltpu.SMEM((1, n), I32)])(
        own, oth, inv, inv_o, blk, blk_o, rhs, rhs_o)
    early = call(functools.partial(early_kernel, n, half, rows), [SMEM] + [VMEM] * 2, [VMEM] * 2, [shape(half * rows, w)] * 2, [pltpu.SMEM((1, n), I32)])(own, x0, blk)
    early = [move(early[m], [((2 * h + 1, h), (2 * h + m, h - 1)) for h in range(1, stages)]) for m in (0, 1)]

    for g in range(stages - 1):
        xs = [move(msg, [((2 * g + m, 0), (2 * (g + d) + m, d - 1)) for m in (0, 1)]) for d in range(1, stages - g)]
        if g:
            acc = move(msg, [((2 * h + m, h - g), (2 * h + m, h - g - 1)) for h in range(g + 1, stages) for m in (0, 1)])
        if g == 1:
            pre_o = other(pre)
        last = g == stages - 2
        more, after = ([acc, pre], [pre_o]) if g else (early, [])
        outs = [shape(n, rows, w)] * 2 if last else [msg_shape]
        scratch = ([pltpu.VMEM(msg_shape.shape, F32)] if last else []) + [pltpu.SMEM((2, n), I32)]
        got = call(functools.partial(step_kernel, n, half, rows, g, len(xs), last), [SMEM] * 2 + [VMEM] * (len(xs) + 9 + len(after)), [VMEM] * len(outs), outs, scratch)(
            own, oth, *xs, *more, msg, inv, inv_o, blk, blk_o, rhs, rhs_o, *after)
        msg = got[0]

    mine, theirs = got
    solved = mine + other(theirs)
    zs = [solved] + [move(solved, [((l, 0), (l, q)) for l in range(levels)]) for q in range(1, planes)]
    out, = call(pick_kernel, [VMEM] * planes, [HBM], [shape(n, rows, w)], [pltpu.SemaphoreType.DMA])(
        *zs)
    return out


def solution(mesh):
    return jax.shard_map(
        solve,
        mesh=mesh,
        in_specs=(
            P("level", None, None),
            P("level", None, None),
            P("level", "row", None, None),
            P("level", "row"),
        ),
        out_specs=P("level", None, None),
        check_vma=False,
    )
```
